32 devices in a mesh: gx: 4 (over z), gy: 8 (over y, x, core).
Axes of the slice: x: 2, y: 2, z: 4, core: 2. Of those that a mesh axis runs over, the one named last changes fastest.
Arguments:
- conductivity: bfloat16 [2, 1024, 4096], P(None, 'gy', 'gx'), may hold values from 0.099609375 to 1.59375
Outputs:
- coarse_stencil: float32 [9, 8, 64, 2048], P(None, 'gy', 'gx')
The draws below stay inside these ranges and needn't reach their ends.
All inputs are finite; a program needn't handle non-finite values.
Results may differ from the reference program's by a relative error of at most 0.0003.
Values may be sent and summed in bfloat16 or wider, within the bound.
A program may use at most 64 MiB of HBM per device.

```python
import math
import jax
import jax.numpy as jnp
from jax import lax

CY = 128
PLANES = 2
NX = 4096
NY = 1024


def block_levels(own_key, dims, shards, low, largest):
    def one(axis_at, parts):
        heights = jax.random.uniform(jax.random.fold_in(jax.random.fold_in(own_key, 6), axis_at), (parts,), jnp.float32, low / len(shards), largest / len(shards))
        return jnp.repeat(jnp.exp(heights), dims[axis_at] // parts).reshape((-1,) + (1,) * (len(dims) - axis_at - 1))

    gain = one(*shards[0])
    for cut in shards[1:]:
        gain = gain * one(*cut)
    return gain


def setup_inputs(seed: int = 0) -> dict:
    arg_keys = jax.random.split(jax.random.key(seed), 2)
    return {
        "conductivity": jnp.clip(jnp.exp(math.log(1.59375) - 2.7725887 * jax.random.uniform(arg_keys[0], (PLANES, NY, NX), jnp.float32) ** block_levels(arg_keys[0], (PLANES, NY, NX), ((1, 8), (2, 4)), -0.2, 0.2)), 0.099609375, 1.59375).astype(jnp.bfloat16),
    }


def harmonic(first, second):
    return 2.0 * first * second / (first + second)


def prepare_window(extended, row_start, col_start, rows_all, cols_all):
    conduct = extended.astype(jnp.float32)
    ext_rows = conduct.shape[1]
    ext_cols = conduct.shape[2]
    row_ids = row_start - 2 + jnp.arange(ext_rows, dtype=jnp.int32)
    col_ids = col_start - 2 + jnp.arange(ext_cols, dtype=jnp.int32)
    row_inside = (row_ids >= 0) & (row_ids < rows_all)
    col_inside = (col_ids >= 0) & (col_ids < cols_all)
    inside = row_inside[:, None] & col_inside[None, :]
    safe_values = jnp.where(inside[None], conduct, 1.0)
    east_face = jnp.where(jnp.roll(inside, -1, 1)[None], harmonic(safe_values, jnp.roll(safe_values, -1, 2)), safe_values)
    west_face = jnp.where(jnp.roll(inside, 1, 1)[None], harmonic(safe_values, jnp.roll(safe_values, 1, 2)), safe_values)
    north_face = jnp.where(jnp.roll(inside, -1, 0)[None], harmonic(safe_values, jnp.roll(safe_values, -1, 1)), safe_values)
    south_face = jnp.where(jnp.roll(inside, 1, 0)[None], harmonic(safe_values, jnp.roll(safe_values, 1, 1)), safe_values)
    vertical = harmonic(safe_values[0], safe_values[1])
    centre = east_face + west_face + north_face + south_face + vertical[None] + safe_values
    col_east = east_face[0] + east_face[1]
    col_west = west_face[0] + west_face[1]
    row_north = north_face[0] + north_face[1]
    row_south = south_face[0] + south_face[1]
    left_weight = col_west / (col_west + col_east)
    right_weight = col_east / (col_west + col_east)
    south_weight = row_south / (row_south + row_north)
    north_weight = row_north / (row_south + row_north)
    odd_rows = (row_ids % 2 == 1)[:, None]
    odd_cols = (col_ids % 2 == 1)[None, :]
    even_point = inside & (row_ids % 2 == 0)[:, None] & (col_ids % 2 == 0)[None, :]
    row_class = ((row_ids // 2) % 3)[:, None]
    col_class = ((col_ids // 2) % 3)[None, :]
    return (inside, odd_rows, odd_cols, even_point, row_class, col_class, east_face, west_face, north_face, south_face, vertical, centre, left_weight, right_weight, south_weight, north_weight)


def probe_sum(prepared, colour):
    (inside, odd_rows, odd_cols, even_point, row_class, col_class, east_face, west_face, north_face, south_face, vertical, centre, left_weight, right_weight, south_weight, north_weight) = prepared
    chosen = even_point & (row_class == colour // 3) & (col_class == colour % 3)
    probe_field = chosen.astype(jnp.float32)
    along_x = jnp.where(odd_cols, left_weight * jnp.roll(probe_field, 1, 1) + right_weight * jnp.roll(probe_field, -1, 1), probe_field)
    fine_field = jnp.where(odd_rows, south_weight * jnp.roll(along_x, 1, 0) + north_weight * jnp.roll(along_x, -1, 0), along_x)
    fine_field = jnp.where(inside, fine_field, 0.0)
    applied = (centre * fine_field - east_face * jnp.roll(fine_field, -1, 1) - west_face * jnp.roll(fine_field, 1, 1)
               - north_face * jnp.roll(fine_field, -1, 0) - south_face * jnp.roll(fine_field, 1, 0) - vertical * fine_field)
    folded = jnp.where(inside, applied[0] + applied[1], 0.0)
    rows_done = folded + jnp.roll(south_weight * folded, -1, 0) + jnp.roll(north_weight * folded, 1, 0)
    cols_done = rows_done + jnp.roll(left_weight * rows_done, -1, 1) + jnp.roll(right_weight * rows_done, 1, 1)
    return cols_done[2:-2:2, 2:-2:2]


def by_offset(colours, row_first, col_first):
    count_rows = colours.shape[1]
    count_cols = colours.shape[2]
    coarse_rows = row_first + jnp.arange(count_rows, dtype=jnp.int32)
    coarse_cols = col_first + jnp.arange(count_cols, dtype=jnp.int32)
    fields = []
    for step_row in (-1, 0, 1):
        for step_col in (-1, 0, 1):
            row_group = (coarse_rows + step_row) % 3
            col_group = (coarse_cols + step_col) % 3
            selected = jnp.zeros((count_rows, count_cols), jnp.float32)
            for colour in range(9):
                chosen = (row_group == colour // 3)[:, None] & (col_group == colour % 3)[None, :]
                selected = jnp.where(chosen, colours[colour], selected)
            fields.append(selected)
    return jnp.stack(fields)


def reference(conductivity):
    rows_all = conductivity.shape[1]
    cols_all = conductivity.shape[2]
    padded = jnp.pad(conductivity, ((0, 0), (2, 2), (2, 2)))
    prepared = prepare_window(padded, 0, 0, rows_all, cols_all)

    def one_colour(colour):
        return probe_sum(prepared, colour)

    colours = lax.map(one_colour, jnp.arange(9, dtype=jnp.int32))
    stencil = by_offset(colours, 0, 0)
    band_rows = CY // 2
    return stencil.reshape(9, stencil.shape[1] // band_rows, band_rows, stencil.shape[2])
```

```python
import functools

import jax
import jax.numpy as jnp
from jax import lax
from jax.experimental import pallas as pl
from jax.experimental.pallas import tpu as pltpu
from jax.sharding import PartitionSpec as P

MESH = pl.DeviceIdType.MESH
LANES = 128


def gather_kernel(
    n, m, cells, main, mid, edge, tails, heads, pack, main_send, main_recv, mid_send, mid_recv, edge_send, edge_recv, own
):
    i = lax.axis_index("gx")
    j = lax.axis_index("gy")
    band = main.shape[2]
    takes_south = (i == 0) & (j > 0)
    takes_north = (i == n - 1) & (j < m - 1)
    before = jnp.maximum(j - 1, 0)
    after = jnp.minimum(j + 1, m - 1)

    barrier = pltpu.get_barrier_semaphore()

    def greet(x, y):
        pl.semaphore_signal(barrier, inc=1, device_id=(x, y), device_id_type=MESH)

    for d in range(1, n):
        greet(lax.rem(i + d, n), j)

    @pl.when(takes_south)
    def _():
        for k in range(n):
            greet(k, before)

    @pl.when(takes_north)
    def _():
        for k in range(n):
            greet(k, after)

    loads = []
    for t in range(n):
        loads.append(pltpu.make_async_copy(cells.at[:, pl.ds(t * band + band - 8, 8), :], tails.at[t], own.at[2 * t]))
        loads.append(pltpu.make_async_copy(cells.at[:, pl.ds(t * band, 8), :], heads.at[t], own.at[2 * t + 1]))
    for load in loads:
        load.start()
    for load in loads:
        load.wait()
    sub = lax.broadcasted_iota(jnp.int32, (8, cells.shape[2]), 0)
    for u in range(n + 2):
        under, over = min(max(u - 2, 0), n - 1), min(u, n - 1)
        low = [pltpu.roll(tails[under, p].astype(jnp.float32), 2 + 2 * p, 0) for p in range(2)]
        high = [pltpu.roll(heads[over, p].astype(jnp.float32), 4 + p, 0) for p in range(2)]
        rows = jnp.where(sub < 2, low[0], jnp.where(sub < 4, low[1], jnp.where(sub == 4, high[0], high[1])))
        pack[u] = rows.astype(jnp.bfloat16)

    @pl.when(jnp.logical_not(takes_south | takes_north))
    def _():
        edge[...] = jnp.ones(edge.shape, edge.dtype)

    north, south = jnp.where(j < m - 1, 1, 0), jnp.where(j > 0, 1, 0)
    pl.semaphore_wait(barrier, n - 1 + north + south)

    def remote(src, dst, send, recv, x, y):
        return pltpu.make_async_remote_copy(
            src_ref=src, dst_ref=dst, send_sem=send, recv_sem=recv, device_id=(x, y), device_id_type=MESH
        )

    def rows_of(t):
        return cells.at[:, pl.ds(pl.multiple_of(t * band, band), band), :]

    def main_copy(d):
        t = lax.rem(i + d, n)
        return remote(rows_of(t), main.at[i], main_send.at[d], main_recv.at[i], t, j)

    def mid_copy(d):
        t = lax.rem(i + d, n)
        return remote(pack.at[t + 1], mid.at[i], mid_send.at[d], mid_recv.at[i], t, j)

    def edge_north():
        return remote(pack.at[n + 1], edge.at[i], edge_send.at[0], edge_recv.at[i], 0, after)

    def edge_south():
        return remote(pack.at[0], edge.at[i], edge_send.at[1], edge_recv.at[i], n - 1, before)

    order = [n // 2] + [d for d in range(1, n) if d != n // 2]
    for d in order:
        main_copy(d).start()
    for d in order:
        mid_copy(d).start()

    @pl.when(j < m - 1)
    def _():
        edge_north().start()

    @pl.when(j > 0)
    def _():
        edge_south().start()

    own_main = pltpu.make_async_copy(rows_of(i), main.at[i], own.at[0])
    own_main.start()
    own_mid = pltpu.make_async_copy(pack.at[i + 1], mid.at[i], own.at[1])
    own_mid.start()
    own_main.wait()
    own_mid.wait()
    for d in range(1, n):
        k = lax.rem(i + d, n)
        remote(rows_of(0), main.at[k], main_send.at[d], main_recv.at[k], k, j).wait_recv()
        remote(pack.at[0], mid.at[k], mid_send.at[d], mid_recv.at[k], k, j).wait_recv()

    @pl.when(takes_south | takes_north)
    def _():
        for k in range(n):
            remote(pack.at[0], edge.at[k], edge_send.at[0], edge_recv.at[k], i, after).wait_recv()

    for d in range(1, n):
        main_copy(d).wait_send()
        mid_copy(d).wait_send()

    @pl.when(j < m - 1)
    def _():
        edge_north().wait_send()

    @pl.when(j > 0)
    def _():
        edge_south().wait_send()


def face(x0, y0, x1, y1):
    s0, s1 = x0 + y0, x1 + y1
    return 2.0 * (x0 * y0 * s1 + x1 * y1 * s0) / (s0 * s1)


def with_vertical(sides, wall, k0, k1):
    vertical = 2.0 * (2.0 * k0 * k1 / (k0 + k1))
    return (sides + (wall + vertical)) - vertical


def stencil_kernel(n, m, main, mid, edge, out, cell, weights):
    band = main.shape[2]
    block = main.shape[3]
    half = band // 2
    rows = cell.shape[2]
    tiles = out.shape[2] // LANES
    per_block = block // (2 * LANES)
    i = lax.axis_index("gx")
    j = lax.axis_index("gy")
    first_rows = (i == 0) & (j == 0)
    last_rows = (i == n - 1) & (j == m - 1)

    taken = 2 * band + 16
    want = lax.broadcasted_iota(jnp.int32, (4 * rows, taken), 0)
    have = lax.broadcasted_iota(jnp.int32, (4 * rows, taken), 1)
    group = jnp.where(want >= 3 * rows, 3, jnp.where(want >= 2 * rows, 2, jnp.where(want >= rows, 1, 0)))
    place = want - group * rows
    plane = jnp.where(group >= 2, 1, 0)
    odd = group - 2 * plane
    inside = plane * band + 2 * jnp.where(place < half, place, 0) + odd
    above = jnp.where(odd == 0, 2 * band + jnp.where(i == n - 1, 8, 0) + 4 + plane, plane * band + 1)
    below = 2 * band + jnp.where(i == 0, 8, 0) + 2 * plane + odd
    source = jnp.where(place == half, above, jnp.where(place == rows - 1, below, inside))
    pick_rows = jnp.where(have == source, 1.0, 0.0).astype(jnp.bfloat16)
    fine = lax.broadcasted_iota(jnp.int32, (2 * LANES, 2 * LANES), 0)
    to = lax.broadcasted_iota(jnp.int32, (2 * LANES, 2 * LANES), 1)
    pick_cols = jnp.where(fine == jnp.where(to < LANES, 2 * to, 2 * (to - LANES) + 1), 1.0, 0.0).astype(jnp.bfloat16)

    lane = lax.broadcasted_iota(jnp.int32, (rows, LANES), 1)
    sub = lax.broadcasted_iota(jnp.int32, (rows, LANES), 0)
    bottom = (sub == 0) & first_rows
    top = (sub == half - 1) & last_rows

    def up(x):
        return pltpu.roll(x, rows - 1, 0)

    def down(x):
        return pltpu.roll(x, 1, 0)

    for t in range(tiles):
        k, part = divmod(t, per_block)
        cols = slice(part * 2 * LANES, (part + 1) * 2 * LANES)
        stored = jnp.concatenate(
            [
                main[k, 0, :, cols].astype(jnp.float32),
                main[k, 1, :, cols].astype(jnp.float32),
                mid[k, :, cols].astype(jnp.float32),
                edge[k, :, cols].astype(jnp.float32),
            ],
            axis=0,
        ).astype(jnp.bfloat16)
        picked = jnp.dot(pick_rows, stored, preferred_element_type=jnp.float32).astype(jnp.bfloat16)
        split = jnp.dot(picked, pick_cols, preferred_element_type=jnp.float32)
        a0, c0, a1, c1 = (split[g * rows : (g + 1) * rows, :LANES] for g in range(4))
        b0, d0, b1, d1 = (split[g * rows : (g + 1) * rows, LANES:] for g in range(4))
        for at, value in enumerate((a0, a1, b0, b1, c0, c1, d0, d1)):
            cell[t, at] = value
        v1 = face(a0, c0, a1, c1)
        v2 = jnp.where(top, c0 + c1, face(c0, up(a0), c1, up(a1)))
        total = 1.0 / (v1 + v2)
        north = v2 * total
        weights[t, 0] = v1 * total
        weights[t, 1] = north
        weights[t, 2] = v1 * north
    ones = jnp.ones((rows, LANES), jnp.float32)
    for at in range(8):
        cell[tiles, at] = ones
    for at in range(3):
        weights[tiles, at] = ones

    def step(t, carry):
        last = (lane == LANES - 1) & (t == tiles - 1)
        first = (lane == 0) & (t == 0)

        def ahead(ref, at):
            return pltpu.roll(jnp.where(lane == 0, ref[t + 1, at], ref[t, at]), LANES - 1, 1)

        rolled = []

        def behind(x):
            turned = pltpu.roll(x, 1, 1)
            before = carry[len(rolled)]
            rolled.append(turned)
            return jnp.where(lane == 0, before, turned)

        a0, a1, b0, b1, c0, c1, d0, d1 = (cell[t, at] for at in range(8))
        s0, n0, t0 = (weights[t, at] for at in range(3))
        wall_a, wall_b, wall_c, wall_d = a0 + a1, b0 + b1, c0 + c1, d0 + d1
        h1 = face(a0, b0, a1, b1)
        h2 = jnp.where(last, wall_b, face(b0, ahead(cell, 0), b1, ahead(cell, 1)))
        g1 = face(c0, d0, c1, d1)
        g2 = jnp.where(last, wall_d, face(d0, ahead(cell, 4), d1, ahead(cell, 5)))
        w1 = face(b0, d0, b1, d1)
        w2 = jnp.where(top, wall_d, face(d0, up(b0), d1, up(b1)))
        total = 1.0 / (w1 + w2)
        s1 = w1 * total
        n1 = w2 * total
        t1 = w1 * n1
        total = 1.0 / (h1 + h2)
        left = h1 * total
        right = h2 * total
        left_up = up(left)
        right_up = up(right)
        s0_next = ahead(weights, 0)
        n0_next = ahead(weights, 1)

        side_a = with_vertical(h1 + jnp.where(first, wall_a, behind(h2)), wall_a, a0, a1)
        side_c = with_vertical(g1 + jnp.where(first, wall_c, behind(g2)), wall_c, c0, c1)
        side_b = with_vertical(h1 + h2, wall_b, b0, b1)
        side_d = with_vertical(g1 + g2, wall_d, d0, d1)

        nc = n0 * side_c
        sc = s0 * side_c
        nd = n1 * side_d
        sd = s1 * side_d
        even = side_a + t0 + s0 * sc + jnp.where(bottom, wall_a, down(t0 + n0 * nc))
        odd_ = side_b + t1 + s1 * sd + jnp.where(bottom, wall_b, down(t1 + n1 * nd))
        even_up = s0 * nc - t0
        odd_up = s1 * nd - t1
        sg = s0 * g1
        ng = n0 * g1
        sq = s0_next * g2
        nq = n0_next * g2
        p = h1 + s1 * sg + jnp.where(bottom, 0.0, down(n1 * ng))
        q = h2 + s1 * sq + jnp.where(bottom, 0.0, down(n1 * nq))
        p_up = n1 * sg
        p_down = s1 * ng
        q_up = s1 * nq
        q_down = n1 * sq

        mid = left * odd_ - p
        east = jnp.where(last, 0.0, right * mid - left * q)
        centre = even + left * (mid - p) + behind(right * (right * odd_ - 2.0 * q))
        lo = left * odd_up - p_up
        ro = right * odd_up - q_down
        north = even_up + left_up * lo - left * p_down + behind(right_up * ro - right * q_up)
        north = jnp.where(top, 0.0, north)
        north_east = jnp.where(last | top, 0.0, right_up * lo - left * q_up)
        north_west = jnp.where(last | top, 0.0, left_up * ro - right * p_down)
        west = behind(east)
        ne_back = behind(north_east)
        nw_back = behind(north_west)
        cols = pl.ds(pl.multiple_of(t * LANES, LANES), LANES)

        def below(x):
            return jnp.where(bottom, 0.0, down(x))

        for at, value in enumerate(
            (below(ne_back), below(north), below(north_west), west, centre, east, nw_back, north, north_east)
        ):
            out[at, :, cols] = value[:half]
        return tuple(rolled)

    zero = jnp.zeros((rows, LANES), jnp.float32)
    lax.fori_loop(0, tiles, step, (zero,) * 7)


def shards(n, m, conductivity):
    planes, local_rows, local_cols = conductivity.shape
    band = local_rows // n
    half = band // 2
    rows = -(-(half + 2) // 8) * 8
    tiles = n * local_cols // (2 * LANES)
    vmem = pl.BlockSpec(memory_space=pltpu.VMEM)
    anywhere = pl.BlockSpec(memory_space=pl.ANY)
    dma = pltpu.SemaphoreType.DMA
    main, mid, edge = pl.pallas_call(
        functools.partial(gather_kernel, n, m),
        out_shape=(
            jax.ShapeDtypeStruct((n, planes, band, local_cols), jnp.bfloat16),
            jax.ShapeDtypeStruct((n, 8, local_cols), jnp.bfloat16),
            jax.ShapeDtypeStruct((n, 8, local_cols), jnp.bfloat16),
        ),
        in_specs=[anywhere],
        out_specs=(vmem, vmem, vmem),
        scratch_shapes=[
            pltpu.VMEM((n, planes, 8, local_cols), jnp.bfloat16),
            pltpu.VMEM((n, planes, 8, local_cols), jnp.bfloat16),
            pltpu.VMEM((n + 2, 8, local_cols), jnp.bfloat16),
            dma((n,)),
            dma((n,)),
            dma((n,)),
            dma((n,)),
            dma((2,)),
            dma((n,)),
            dma((2 * n,)),
        ],
        compiler_params=pltpu.CompilerParams(collective_id=0, has_side_effects=True),
        name="gather_rows",
    )(conductivity)
    stencil = pl.pallas_call(
        functools.partial(stencil_kernel, n, m),
        out_shape=jax.ShapeDtypeStruct((9, half, tiles * LANES), jnp.float32),
        in_specs=[vmem, vmem, vmem],
        out_specs=vmem,
        scratch_shapes=[
            pltpu.VMEM((tiles + 1, 8, rows, LANES), jnp.float32),
            pltpu.VMEM((tiles + 1, 3, rows, LANES), jnp.float32),
        ],
        name="stencil",
    )(main, mid, edge)
    return stencil[:, None]


def solution(mesh):
    n, m = mesh.shape["gx"], mesh.shape["gy"]
    return jax.shard_map(
        functools.partial(shards, n, m),
        mesh=mesh,
        in_specs=(P(None, "gy", "gx"),),
        out_specs=P(None, "gy", "gx", None),
        check_vma=False,
    )
```

```python
import functools

import jax
import jax.numpy as jnp
from jax import lax
from jax.experimental import pallas as pl
from jax.experimental.pallas import tpu as pltpu
from jax.sharding import PartitionSpec as P

MESH = pl.DeviceIdType.MESH
LANES = 128


def coarse_kernel(
    n, m, cells, out, main, mid, edge, tails, heads, pack, fields,
    main_send, main_recv, mid_send, mid_recv, edge_send, edge_recv, own,
):
    i = lax.axis_index("gx")
    j = lax.axis_index("gy")
    band = main.shape[2]
    takes_south = (i == 0) & (j > 0)
    takes_north = (i == n - 1) & (j < m - 1)
    before = jnp.maximum(j - 1, 0)
    after = jnp.minimum(j + 1, m - 1)

    barrier = pltpu.get_barrier_semaphore()

    def greet(x, y):
        pl.semaphore_signal(barrier, inc=1, device_id=(x, y), device_id_type=MESH)

    for d in range(1, n):
        greet(lax.rem(i + d, n), j)

    @pl.when(takes_south)
    def _():
        for k in range(n):
            greet(k, before)

    @pl.when(takes_north)
    def _():
        for k in range(n):
            greet(k, after)

    def rows_of(t):
        return cells.at[:, pl.ds(pl.multiple_of(t * band, band), band), :]

    own_main = pltpu.make_async_copy(rows_of(i), main.at[i], own.at[2 * n])
    own_main.start()

    loads = []
    for t in range(n):
        loads.append(pltpu.make_async_copy(cells.at[:, pl.ds(t * band + band - 8, 8), :], tails.at[t], own.at[2 * t]))
        loads.append(pltpu.make_async_copy(cells.at[:, pl.ds(t * band, 8), :], heads.at[t], own.at[2 * t + 1]))
    for load in loads:
        load.start()
    for load in loads:
        load.wait()
    sub = lax.broadcasted_iota(jnp.int32, (8, cells.shape[2]), 0)
    for u in range(n + 2):
        under, over = min(max(u - 2, 0), n - 1), min(u, n - 1)
        low = [pltpu.roll(tails[under, p].astype(jnp.float32), 2 + 2 * p, 0) for p in range(2)]
        high = [pltpu.roll(heads[over, p].astype(jnp.float32), 4 + p, 0) for p in range(2)]
        rows = jnp.where(sub < 2, low[0], jnp.where(sub < 4, low[1], jnp.where(sub == 4, high[0], high[1])))
        pack[u] = rows.astype(jnp.bfloat16)

    @pl.when(jnp.logical_not(takes_south | takes_north))
    def _():
        edge[...] = jnp.ones(edge.shape, edge.dtype)

    north, south = jnp.where(j < m - 1, 1, 0), jnp.where(j > 0, 1, 0)
    pl.semaphore_wait(barrier, n - 1 + north + south)

    def remote(src, dst, send, recv, x, y):
        return pltpu.make_async_remote_copy(
            src_ref=src, dst_ref=dst, send_sem=send, recv_sem=recv, device_id=(x, y), device_id_type=MESH
        )

    turn = jnp.where(i < n // 2, 1, n - 1)

    def peer(d):
        return lax.rem(i + turn * d, n)

    def main_copy(d):
        t = peer(d)
        return remote(rows_of(t), main.at[i], main_send.at[d], main_recv.at[i], t, j)

    def mid_copy(d):
        t = peer(d)
        return remote(pack.at[t + 1], mid.at[i], mid_send.at[d], mid_recv.at[i], t, j)

    def edge_north():
        return remote(pack.at[n + 1], edge.at[i], edge_send.at[0], edge_recv.at[i], 0, after)

    def edge_south():
        return remote(pack.at[0], edge.at[i], edge_send.at[1], edge_recv.at[i], n - 1, before)

    order = [n // 2] + [d for d in range(1, n) if d != n // 2]
    for d in order:
        mid_copy(d).start()

    @pl.when(j < m - 1)
    def _():
        edge_north().start()

    @pl.when(j > 0)
    def _():
        edge_south().start()

    for d in order:
        main_copy(d).start()
    own_mid = pltpu.make_async_copy(pack.at[i + 1], mid.at[i], own.at[1])
    own_mid.start()

    def edge_arrived(k):
        @pl.when(takes_south | takes_north)
        def _():
            remote(pack.at[0], edge.at[k], edge_send.at[0], edge_recv.at[k], i, after).wait_recv()

    first, second = stages(n, m, main, mid, edge, out, fields)
    own_main.wait()
    own_mid.wait()
    edge_arrived(i)
    first(i)
    for d in order:
        k = peer(d)
        remote(pack.at[0], mid.at[k], mid_send.at[d], mid_recv.at[k], k, j).wait_recv()
        edge_arrived(k)
        remote(rows_of(0), main.at[k], main_send.at[d], main_recv.at[k], k, j).wait_recv()
        first(k)
    second()

    for d in order:
        main_copy(d).wait_send()
        mid_copy(d).wait_send()

    @pl.when(j < m - 1)
    def _():
        edge_north().wait_send()

    @pl.when(j > 0)
    def _():
        edge_south().wait_send()


def face(x0, y0, x1, y1):
    s0, s1 = x0 + y0, x1 + y1
    return 2.0 * (x0 * y0 * s1 + x1 * y1 * s0) / (s0 * s1)


def middle(one, two):
    total = 1.0 / (one + two)
    second = two * total
    return one * total, second, one * second


def with_vertical(sides, k0, k1):
    vertical = 2.0 * (2.0 * k0 * k1 / (k0 + k1))
    return (sides + ((k0 + k1) + vertical)) - vertical


def stages(n, m, main, mid, edge, out, fields):
    band = main.shape[2]
    block = main.shape[3]
    half = band // 2
    rows = fields.shape[2]
    tiles = out.shape[2] // LANES
    per_block = block // (2 * LANES)
    i = lax.axis_index("gx")
    j = lax.axis_index("gy")
    first_rows = (i == 0) & (j == 0)
    last_rows = (i == n - 1) & (j == m - 1)

    taken = 2 * band + 16
    want = lax.broadcasted_iota(jnp.int32, (4 * rows, taken), 0)
    have = lax.broadcasted_iota(jnp.int32, (4 * rows, taken), 1)
    group = jnp.where(want >= 3 * rows, 3, jnp.where(want >= 2 * rows, 2, jnp.where(want >= rows, 1, 0)))
    place = want - group * rows
    plane = jnp.where(group >= 2, 1, 0)
    odd = group - 2 * plane
    inside = plane * band + 2 * jnp.where(place < half, place, 0) + odd
    above = jnp.where(odd == 0, 2 * band + jnp.where(i == n - 1, 8, 0) + 4 + plane, plane * band + 1)
    below = 2 * band + jnp.where(i == 0, 8, 0) + 2 * plane + odd
    source = jnp.where(place == half, above, jnp.where(place == rows - 1, below, inside))
    pick_rows = jnp.where(have == source, 1.0, 0.0).astype(jnp.bfloat16)
    fine = lax.broadcasted_iota(jnp.int32, (2 * LANES, 2 * LANES), 0)
    to = lax.broadcasted_iota(jnp.int32, (2 * LANES, 2 * LANES), 1)
    pick_cols = jnp.where(fine == jnp.where(to < LANES, 2 * to, 2 * (to - LANES) + 1), 1.0, 0.0).astype(jnp.bfloat16)

    lane = lax.broadcasted_iota(jnp.int32, (rows, LANES), 1)
    sub = lax.broadcasted_iota(jnp.int32, (rows, LANES), 0)
    bottom = (sub == 0) & first_rows
    top = (sub == half - 1) & last_rows

    def up(x):
        return pltpu.roll(x, rows - 1, 0)

    def down(x):
        return pltpu.roll(x, 1, 0)

    def tile_terms(k, part):
        t = k * per_block + part
        cols = pl.ds(pl.multiple_of(part * 2 * LANES, 2 * LANES), 2 * LANES)
        stored = jnp.concatenate(
            [
                main[k, 0, :, cols].astype(jnp.float32),
                main[k, 1, :, cols].astype(jnp.float32),
                mid[k, :, cols].astype(jnp.float32),
                edge[k, :, cols].astype(jnp.float32),
            ],
            axis=0,
        ).astype(jnp.bfloat16)
        picked = jnp.dot(pick_rows, stored, preferred_element_type=jnp.float32).astype(jnp.bfloat16)
        split = jnp.dot(picked, pick_cols, preferred_element_type=jnp.float32)
        a0, c0, a1, c1 = (split[g * rows : (g + 1) * rows, :LANES] for g in range(4))
        b0, d0, b1, d1 = (split[g * rows : (g + 1) * rows, LANES:] for g in range(4))
        s0, n0, t0 = middle(face(a0, c0, a1, c1), jnp.where(top, c0 + c1, face(c0, up(a0), c1, up(a1))))
        s1, n1, t1 = middle(face(b0, d0, b1, d1), jnp.where(top, d0 + d1, face(d0, up(b0), d1, up(b1))))
        h1 = face(a0, b0, a1, b1)
        g1 = face(c0, d0, c1, d1)
        side_a = with_vertical(h1, a0, a1)
        side_b = with_vertical(h1, b0, b1)
        side_c = with_vertical(g1, c0, c1)
        side_d = with_vertical(g1, d0, d1)
        for at, value in enumerate(
            (a0, a1, c0, c1, s0, n0, b0, b1, d0, d1, t0, s1, n1, t1, h1, g1, side_a, side_b, side_c, side_d)
        ):
            fields[t, at] = value

    def first(k):
        lax.fori_loop(0, per_block, lambda part, carry: (tile_terms(k, part), carry)[1], 0)

    ones = jnp.ones((rows, LANES), jnp.float32)
    for at in range(6):
        fields[tiles, at] = ones

    def step(t, carry):
        last = (lane == LANES - 1) & (t == tiles - 1)
        first_lane = (lane == 0) & (t == 0)

        def ahead(at):
            return pltpu.roll(jnp.where(lane == 0, fields[t + 1, at], fields[t, at]), LANES - 1, 1)

        rolled = []

        def behind(x):
            turned = pltpu.roll(x, 1, 1)
            before = carry[len(rolled)]
            rolled.append(turned)
            return jnp.where(lane == 0, before, turned)

        a0, a1, c0, c1, s0, n0, b0, b1, d0, d1 = (fields[t, at] for at in range(10))
        t0, s1, n1, t1, h1, g1, side_a, side_b, side_c, side_d = (fields[t, at] for at in range(10, 20))
        wall_a, wall_b = a0 + a1, b0 + b1
        h2 = jnp.where(last, wall_b, face(b0, ahead(0), b1, ahead(1)))
        g2 = jnp.where(last, d0 + d1, face(d0, ahead(2), d1, ahead(3)))
        left, right, _ = middle(h1, h2)
        left_up = up(left)
        right_up = up(right)
        s0_next = ahead(4)
        n0_next = ahead(5)
        side_a = side_a + jnp.where(first_lane, wall_a, behind(h2))
        side_c = side_c + jnp.where(first_lane, c0 + c1, behind(g2))
        side_b = side_b + h2
        side_d = side_d + g2

        nc = n0 * side_c
        sc = s0 * side_c
        nd = n1 * side_d
        sd = s1 * side_d
        even = side_a + t0 + s0 * sc + jnp.where(bottom, wall_a, down(t0 + n0 * nc))
        odd_ = side_b + t1 + s1 * sd + jnp.where(bottom, wall_b, down(t1 + n1 * nd))
        even_up = s0 * nc - t0
        odd_up = s1 * nd - t1
        sg = s0 * g1
        ng = n0 * g1
        sq = s0_next * g2
        nq = n0_next * g2
        p = h1 + s1 * sg + jnp.where(bottom, 0.0, down(n1 * ng))
        q = h2 + s1 * sq + jnp.where(bottom, 0.0, down(n1 * nq))
        p_up = n1 * sg
        p_down = s1 * ng
        q_up = s1 * nq
        q_down = n1 * sq

        mid = left * odd_ - p
        east = jnp.where(last, 0.0, right * mid - left * q)
        centre = even + left * (mid - p) + behind(right * (right * odd_ - 2.0 * q))
        lo = left * odd_up - p_up
        ro = right * odd_up - q_down
        north = even_up + left_up * lo - left * p_down + behind(right_up * ro - right * q_up)
        north = jnp.where(top, 0.0, north)
        north_east = jnp.where(last | top, 0.0, right_up * lo - left * q_up)
        north_west = jnp.where(last | top, 0.0, left_up * ro - right * p_down)
        west = behind(east)
        ne_back = behind(north_east)
        nw_back = behind(north_west)
        cols = pl.ds(pl.multiple_of(t * LANES, LANES), LANES)

        def below(x):
            return jnp.where(bottom, 0.0, down(x))

        for at, value in enumerate(
            (below(ne_back), below(north), below(north_west), west, centre, east, nw_back, north, north_east)
        ):
            out[at, :, cols] = value[:half]
        return tuple(rolled)

    def second():
        zero = jnp.zeros((rows, LANES), jnp.float32)
        lax.fori_loop(0, tiles, step, (zero,) * 7)

    return first, second


def shards(n, m, conductivity):
    planes, local_rows, local_cols = conductivity.shape
    band = local_rows // n
    half = band // 2
    rows = -(-(half + 2) // 8) * 8
    tiles = n * local_cols // (2 * LANES)
    vmem = pl.BlockSpec(memory_space=pltpu.VMEM)
    anywhere = pl.BlockSpec(memory_space=pl.ANY)
    dma = pltpu.SemaphoreType.DMA
    stencil = pl.pallas_call(
        functools.partial(coarse_kernel, n, m),
        out_shape=jax.ShapeDtypeStruct((9, half, tiles * LANES), jnp.float32),
        in_specs=[anywhere],
        out_specs=vmem,
        scratch_shapes=[
            pltpu.VMEM((n, planes, band, local_cols), jnp.bfloat16),
            pltpu.VMEM((n, 8, local_cols), jnp.bfloat16),
            pltpu.VMEM((n, 8, local_cols), jnp.bfloat16),
            pltpu.VMEM((n, planes, 8, local_cols), jnp.bfloat16),
            pltpu.VMEM((n, planes, 8, local_cols), jnp.bfloat16),
            pltpu.VMEM((n + 2, 8, local_cols), jnp.bfloat16),
            pltpu.VMEM((tiles + 1, 20, rows, LANES), jnp.float32),
            dma((n,)),
            dma((n,)),
            dma((n,)),
            dma((n,)),
            dma((2,)),
            dma((n,)),
            dma((2 * n + 1,)),
        ],
        compiler_params=pltpu.CompilerParams(
            collective_id=0, has_side_effects=True, vmem_limit_bytes=24 * 1024 * 1024
        ),
        name="coarse",
    )(conductivity)
    return stencil[:, None]


def solution(mesh):
    n, m = mesh.shape["gx"], mesh.shape["gy"]
    return jax.shard_map(
        functools.partial(shards, n, m),
        mesh=mesh,
        in_specs=(P(None, "gy", "gx"),),
        out_specs=P(None, "gy", "gx", None),
        check_vma=False,
    )
```

```python
import functools

import jax
import jax.numpy as jnp
from jax import lax
from jax.experimental import pallas as pl
from jax.experimental.pallas import tpu as pltpu
from jax.sharding import PartitionSpec as P

MESH = pl.DeviceIdType.MESH
LANES = 128
UNROLL = 4
STEPS = 4
VMEM_LIMIT = 16 * 1024 * 1024


def coarse_kernel(
    n, m, cells, fields, main, mid, edge, tails, heads, pack,
    main_send, main_recv, mid_send, mid_recv, edge_send, edge_recv, own,
):
    i = lax.axis_index("gx")
    j = lax.axis_index("gy")
    band = main.shape[2]
    takes_south = (i == 0) & (j > 0)
    takes_north = (i == n - 1) & (j < m - 1)
    before = jnp.maximum(j - 1, 0)
    after = jnp.minimum(j + 1, m - 1)

    barrier = pltpu.get_barrier_semaphore()

    def greet(x, y):
        pl.semaphore_signal(barrier, inc=1, device_id=(x, y), device_id_type=MESH)

    for d in range(1, n):
        greet(lax.rem(i + d, n), j)

    @pl.when(takes_south)
    def _():
        for k in range(n):
            greet(k, before)

    @pl.when(takes_north)
    def _():
        for k in range(n):
            greet(k, after)

    def rows_of(t):
        return cells.at[:, pl.ds(pl.multiple_of(t * band, band), band), :]

    own_main = pltpu.make_async_copy(rows_of(i), main.at[i], own.at[2 * n])
    own_main.start()

    loads = []
    for t in range(n):
        loads.append(pltpu.make_async_copy(cells.at[:, pl.ds(t * band + band - 8, 8), :], tails.at[t], own.at[2 * t]))
        loads.append(pltpu.make_async_copy(cells.at[:, pl.ds(t * band, 8), :], heads.at[t], own.at[2 * t + 1]))
    for load in loads:
        load.start()
    for load in loads:
        load.wait()
    sub = lax.broadcasted_iota(jnp.int32, (8, cells.shape[2]), 0)
    for u in range(n + 2):
        under, over = min(max(u - 2, 0), n - 1), min(u, n - 1)
        low = [pltpu.roll(tails[under, p].astype(jnp.float32), 2 + 2 * p, 0) for p in range(2)]
        high = [pltpu.roll(heads[over, p].astype(jnp.float32), 4 + p, 0) for p in range(2)]
        rows = jnp.where(sub < 2, low[0], jnp.where(sub < 4, low[1], jnp.where(sub == 4, high[0], high[1])))
        pack[u] = rows.astype(jnp.bfloat16)

    @pl.when(jnp.logical_not(takes_south | takes_north))
    def _():
        edge[...] = jnp.ones(edge.shape, edge.dtype)

    north, south = jnp.where(j < m - 1, 1, 0), jnp.where(j > 0, 1, 0)
    pl.semaphore_wait(barrier, n - 1 + north + south)

    def remote(src, dst, send, recv, x, y):
        return pltpu.make_async_remote_copy(
            src_ref=src, dst_ref=dst, send_sem=send, recv_sem=recv, device_id=(x, y), device_id_type=MESH
        )

    turn = jnp.where(i < n // 2, 1, n - 1)

    def peer(d):
        return lax.rem(i + turn * d, n)

    def main_copy(d):
        t = peer(d)
        return remote(rows_of(t), main.at[i], main_send.at[d], main_recv.at[i], t, j)

    def mid_copy(d):
        t = peer(d)
        return remote(pack.at[t + 1], mid.at[i], mid_send.at[d], mid_recv.at[i], t, j)

    def edge_north():
        return remote(pack.at[n + 1], edge.at[i], edge_send.at[0], edge_recv.at[i], 0, after)

    def edge_south():
        return remote(pack.at[0], edge.at[i], edge_send.at[1], edge_recv.at[i], n - 1, before)

    order = list(range(n - 1, 0, -1))
    for d in order:
        mid_copy(d).start()

    @pl.when(j < m - 1)
    def _():
        edge_north().start()

    @pl.when(j > 0)
    def _():
        edge_south().start()

    for d in order:
        main_copy(d).start()
    own_mid = pltpu.make_async_copy(pack.at[i + 1], mid.at[i], own.at[1])
    own_mid.start()

    def edge_arrived(k):
        @pl.when(takes_south | takes_north)
        def _():
            remote(pack.at[0], edge.at[k], edge_send.at[0], edge_recv.at[k], i, after).wait_recv()

    first = arrival_stage(n, m, main, mid, edge, fields)
    own_main.wait()
    own_mid.wait()
    edge_arrived(i)
    first(i)
    for d in order:
        k = peer(d)
        remote(pack.at[0], mid.at[k], mid_send.at[d], mid_recv.at[k], k, j).wait_recv()
        edge_arrived(k)
        remote(rows_of(0), main.at[k], main_send.at[d], main_recv.at[k], k, j).wait_recv()
        first(k)

    for d in order:
        main_copy(d).wait_send()
        mid_copy(d).wait_send()

    @pl.when(j < m - 1)
    def _():
        edge_north().wait_send()

    @pl.when(j > 0)
    def _():
        edge_south().wait_send()


def parts(x0, y0, x1, y1):
    s0, s1 = x0 + y0, x1 + y1
    return x0 * y0 * s1 + x1 * y1 * s0, s0 * s1


def two_faces(one, two):
    scale = 2.0 / (one[1] * two[1])
    return one[0] * two[1] * scale, two[0] * one[1] * scale


def middle(one, two):
    x, y = one[0] * two[1], two[0] * one[1]
    total = 1.0 / (x + y)
    return x * total, y * total, 2.0 * (one[0] * two[0]) * total


def verticals(pairs):
    sums = [x + y for x, y in pairs]
    low, high = sums[0] * sums[1], sums[2] * sums[3]
    scale = 4.0 / (low * high)
    low, high = high * scale, low * scale
    shares = (sums[1] * low, sums[0] * low, sums[3] * high, sums[2] * high)
    return [x * y * share for (x, y), share in zip(pairs, shares)]


def arrival_stage(n, m, main, mid, edge, fields):
    band = main.shape[2]
    block = main.shape[3]
    half = band // 2
    rows = fields.shape[2]
    tiles = fields.shape[0] - 1
    per_block = block // (2 * LANES)
    i = lax.axis_index("gx")
    j = lax.axis_index("gy")
    last_rows = (i == n - 1) & (j == m - 1)

    taken = 2 * band + 16
    want = lax.broadcasted_iota(jnp.int32, (4 * rows, taken), 0)
    have = lax.broadcasted_iota(jnp.int32, (4 * rows, taken), 1)
    group = jnp.where(want >= 3 * rows, 3, jnp.where(want >= 2 * rows, 2, jnp.where(want >= rows, 1, 0)))
    place = want - group * rows
    plane = jnp.where(group >= 2, 1, 0)
    odd = group - 2 * plane
    inside = plane * band + 2 * jnp.where(place < half, place, 0) + odd
    above = jnp.where(odd == 0, 2 * band + jnp.where(i == n - 1, 8, 0) + 4 + plane, plane * band + 1)
    below = 2 * band + jnp.where(i == 0, 8, 0) + 2 * plane + odd
    source = jnp.where(place == half, above, jnp.where(place == rows - 1, below, inside))
    pick_rows = jnp.where(have == source, 1.0, 0.0).astype(jnp.bfloat16)
    fine = lax.broadcasted_iota(jnp.int32, (2 * LANES, 2 * LANES), 0)
    to = lax.broadcasted_iota(jnp.int32, (2 * LANES, 2 * LANES), 1)
    pick_cols = jnp.where(fine == jnp.where(to < LANES, 2 * to, 2 * (to - LANES) + 1), 1.0, 0.0).astype(jnp.bfloat16)

    top = (lax.broadcasted_iota(jnp.int32, (rows, LANES), 0) == half - 1) & last_rows

    def up(x):
        return pltpu.roll(x, rows - 1, 0)

    def tile_terms(k, part):
        t = k * per_block + part
        cols = pl.ds(pl.multiple_of(part * 2 * LANES, 2 * LANES), 2 * LANES)
        stored = jnp.concatenate(
            [
                main[k, 0, :, cols].astype(jnp.float32),
                main[k, 1, :, cols].astype(jnp.float32),
                mid[k, :, cols].astype(jnp.float32),
                edge[k, :, cols].astype(jnp.float32),
            ],
            axis=0,
        ).astype(jnp.bfloat16)
        picked = jnp.dot(pick_rows, stored, preferred_element_type=jnp.float32).astype(jnp.bfloat16)
        split = jnp.dot(picked, pick_cols, preferred_element_type=jnp.float32)
        a0, c0, a1, c1 = (split[g * rows : (g + 1) * rows, :LANES] for g in range(4))
        b0, d0, b1, d1 = (split[g * rows : (g + 1) * rows, LANES:] for g in range(4))
        def wall(x0, x1, inner):
            return jnp.where(top, 0.5 * (x0 + x1), inner[0]), jnp.where(top, 1.0, inner[1])

        s0, n0, t0 = middle(parts(a0, c0, a1, c1), wall(c0, c1, parts(c0, up(a0), c1, up(a1))))
        s1, n1, t1 = middle(parts(b0, d0, b1, d1), wall(d0, d1, parts(d0, up(b0), d1, up(b1))))
        h1, g1 = two_faces(parts(a0, b0, a1, b1), parts(c0, d0, c1, d1))
        pairs = ((a0, a1), (b0, b1), (c0, c1), (d0, d1))
        side_a, side_b, side_c, side_d = (
            (x + ((k0 + k1) + v)) - v for x, (k0, k1), v in zip((h1, h1, g1, g1), pairs, verticals(pairs))
        )
        for at, value in enumerate(
            (a0, a1, c0, c1, s0, n0, b0, b1, d0, d1, t0, s1, n1, t1, h1, g1, side_a, side_b, side_c, side_d)
        ):
            fields[t, at] = value

    def first(k):
        lax.fori_loop(0, per_block, lambda part, carry: (tile_terms(k, part), carry)[1], 0, unroll=UNROLL)

    ones = jnp.ones((rows, LANES), jnp.float32)
    for at in range(6):
        fields[tiles, at] = ones

    return first


def stencil_kernel(n, m, half, chunk, fields, out, held, sent):
    rows = fields.shape[2]
    tiles = fields.shape[0] - 1
    i = lax.axis_index("gx")
    j = lax.axis_index("gy")
    lane = lax.broadcasted_iota(jnp.int32, (rows, LANES), 1)
    sub = lax.broadcasted_iota(jnp.int32, (rows, LANES), 0)
    bottom = (sub == 0) & (i == 0) & (j == 0)
    top = (sub == half - 1) & (i == n - 1) & (j == m - 1)

    def up(x):
        return pltpu.roll(x, rows - 1, 0)

    def down(x):
        return pltpu.roll(x, 1, 0)

    def step(t, carry):
        last = (lane == LANES - 1) & (t == tiles - 1)
        first_lane = (lane == 0) & (t == 0)

        def ahead(at):
            return pltpu.roll(jnp.where(lane == 0, fields[t + 1, at], fields[t, at]), LANES - 1, 1)

        rolled = []

        def behind(x):
            turned = pltpu.roll(x, 1, 1)
            before = carry[len(rolled)]
            rolled.append(turned)
            return jnp.where(lane == 0, before, turned)

        a0, a1, c0, c1, s0, n0, b0, b1, d0, d1 = (fields[t, at] for at in range(10))
        t0, s1, n1, t1, h1, g1, side_a, side_b, side_c, side_d = (fields[t, at] for at in range(10, 20))
        wall_a, wall_b = a0 + a1, b0 + b1
        h2, g2 = two_faces(parts(b0, ahead(0), b1, ahead(1)), parts(d0, ahead(2), d1, ahead(3)))
        h2 = jnp.where(last, wall_b, h2)
        g2 = jnp.where(last, d0 + d1, g2)
        total = 1.0 / (h1 + h2)
        left, right = h1 * total, h2 * total
        left_up = up(left)
        right_up = up(right)
        s0_next = ahead(4)
        n0_next = ahead(5)
        side_a = side_a + jnp.where(first_lane, wall_a, behind(h2))
        side_c = side_c + jnp.where(first_lane, c0 + c1, behind(g2))
        side_b = side_b + h2
        side_d = side_d + g2

        nc = n0 * side_c
        sc = s0 * side_c
        nd = n1 * side_d
        sd = s1 * side_d
        even = side_a + t0 + s0 * sc + jnp.where(bottom, wall_a, down(t0 + n0 * nc))
        odd_ = side_b + t1 + s1 * sd + jnp.where(bottom, wall_b, down(t1 + n1 * nd))
        even_up = s0 * nc - t0
        odd_up = s1 * nd - t1
        sg = s0 * g1
        ng = n0 * g1
        sq = s0_next * g2
        nq = n0_next * g2
        p = h1 + s1 * sg + jnp.where(bottom, 0.0, down(n1 * ng))
        q = h2 + s1 * sq + jnp.where(bottom, 0.0, down(n1 * nq))
        p_up = n1 * sg
        p_down = s1 * ng
        q_up = s1 * nq
        q_down = n1 * sq

        mid = left * odd_ - p
        east = jnp.where(last, 0.0, right * mid - left * q)
        centre = even + left * (mid - p) + behind(right * (right * odd_ - 2.0 * q))
        lo = left * odd_up - p_up
        ro = right * odd_up - q_down
        north = even_up + left_up * lo - left * p_down + behind(right_up * ro - right * q_up)
        north = jnp.where(top, 0.0, north)
        north_east = jnp.where(last | top, 0.0, right_up * lo - left * q_up)
        north_west = jnp.where(last | top, 0.0, left_up * ro - right * p_down)
        west = behind(east)
        ne_back = behind(north_east)
        nw_back = behind(north_west)
        cols = pl.ds(pl.multiple_of(t * LANES, LANES), LANES)

        def below(x):
            return jnp.where(bottom, 0.0, down(x))

        for at, value in enumerate(
            (below(ne_back), below(north), below(north_west), west, centre, east, nw_back, north, north_east)
        ):
            held[at, :, cols] = value[:half]
        return tuple(rolled)

    def leave(c):
        cols = pl.ds(c * chunk * LANES, chunk * LANES)
        return pltpu.make_async_copy(held.at[:, :, cols], out.at[:, :, cols], sent.at[c])

    carry = (jnp.zeros((rows, LANES), jnp.float32),) * 7
    for c in range(tiles // chunk):
        carry = lax.fori_loop(c * chunk, (c + 1) * chunk, step, carry, unroll=STEPS)
        leave(c).start()
    for c in range(tiles // chunk):
        leave(c).wait()


def shards(n, m, conductivity):
    planes, local_rows, local_cols = conductivity.shape
    band = local_rows // n
    half = band // 2
    rows = -(-(half + 2) // 8) * 8
    tiles = n * local_cols // (2 * LANES)
    vmem = pl.BlockSpec(memory_space=pltpu.VMEM)
    anywhere = pl.BlockSpec(memory_space=pl.ANY)
    dma = pltpu.SemaphoreType.DMA
    shape = (tiles + 1, 20, rows, LANES)
    fields = pl.pallas_call(
        functools.partial(coarse_kernel, n, m),
        out_shape=jax.ShapeDtypeStruct(shape, jnp.float32),
        in_specs=[anywhere],
        out_specs=vmem,
        scratch_shapes=[
            pltpu.VMEM((n, planes, band, local_cols), jnp.bfloat16),
            pltpu.VMEM((n, 8, local_cols), jnp.bfloat16),
            pltpu.VMEM((n, 8, local_cols), jnp.bfloat16),
            pltpu.VMEM((n, planes, 8, local_cols), jnp.bfloat16),
            pltpu.VMEM((n, planes, 8, local_cols), jnp.bfloat16),
            pltpu.VMEM((n + 2, 8, local_cols), jnp.bfloat16),
            dma((n,)),
            dma((n,)),
            dma((n,)),
            dma((n,)),
            dma((2,)),
            dma((n,)),
            dma((2 * n + 1,)),
        ],
        compiler_params=pltpu.CompilerParams(
            collective_id=0, has_side_effects=True, vmem_limit_bytes=VMEM_LIMIT
        ),
        name="coarse",
    )(pltpu.with_memory_space_constraint(conductivity, pltpu.HBM))
    chunk = tiles // 4
    stencil = pl.pallas_call(
        functools.partial(stencil_kernel, n, m, half, chunk),
        out_shape=jax.ShapeDtypeStruct((9, half, tiles * LANES), jnp.float32),
        in_specs=[vmem],
        out_specs=anywhere,
        scratch_shapes=[pltpu.VMEM((9, half, tiles * LANES), jnp.float32), dma((4,))],
        compiler_params=pltpu.CompilerParams(vmem_limit_bytes=VMEM_LIMIT),
        name="stencil",
    )(fields)
    return stencil[:, None]


def solution(mesh):
    n, m = mesh.shape["gx"], mesh.shape["gy"]
    return jax.shard_map(
        functools.partial(shards, n, m),
        mesh=mesh,
        in_specs=(P(None, "gy", "gx"),),
        out_specs=P(None, "gy", "gx", None),
        check_vma=False,
    )
```

```python
import functools

import jax
import jax.numpy as jnp
from jax import lax
from jax.experimental import pallas as pl
from jax.experimental.pallas import tpu as pltpu
from jax.sharding import PartitionSpec as P

MESH = pl.DeviceIdType.MESH
LANES = 128
UNROLL = 4
STEPS = 4
VMEM_LIMIT = 16 * 1024 * 1024


def coarse_kernel(
    n, m, cells, fields, main, mid, edge, tails, heads, pack,
    main_send, main_recv, mid_send, mid_recv, edge_send, edge_recv, own,
):
    i = lax.axis_index("gx")
    j = lax.axis_index("gy")
    band = main.shape[2]
    takes_south = (i == 0) & (j > 0)
    takes_north = (i == n - 1) & (j < m - 1)
    before = jnp.maximum(j - 1, 0)
    after = jnp.minimum(j + 1, m - 1)

    barrier = pltpu.get_barrier_semaphore()

    def greet(x, y):
        pl.semaphore_signal(barrier, inc=1, device_id=(x, y), device_id_type=MESH)

    for d in range(1, n):
        greet(lax.rem(i + d, n), j)

    @pl.when(takes_south)
    def _():
        for k in range(n):
            greet(k, before)

    @pl.when(takes_north)
    def _():
        for k in range(n):
            greet(k, after)

    def rows_of(t):
        return cells.at[:, pl.ds(pl.multiple_of(t * band, band), band), :]

    own_main = pltpu.make_async_copy(rows_of(i), main.at[i], own.at[2 * n])
    own_main.start()

    loads = []
    for t in range(n):
        loads.append(pltpu.make_async_copy(cells.at[:, pl.ds(t * band + band - 8, 8), :], tails.at[t], own.at[2 * t]))
        loads.append(pltpu.make_async_copy(cells.at[:, pl.ds(t * band, 8), :], heads.at[t], own.at[2 * t + 1]))
    for load in loads:
        load.start()
    @pl.when(jnp.logical_not(takes_south | takes_north))
    def _():
        edge[...] = jnp.ones(edge.shape, edge.dtype)

    north, south = jnp.where(j < m - 1, 1, 0), jnp.where(j > 0, 1, 0)
    pl.semaphore_wait(barrier, n - 1 + north + south)

    def remote(src, dst, send, recv, x, y):
        return pltpu.make_async_remote_copy(
            src_ref=src, dst_ref=dst, send_sem=send, recv_sem=recv, device_id=(x, y), device_id_type=MESH
        )

    turn = jnp.where(i < n // 2, 1, n - 1)

    def peer(d):
        return lax.rem(i + turn * d, n)

    def main_copy(d):
        t = peer(d)
        return remote(rows_of(t), main.at[i], main_send.at[d], main_recv.at[i], t, j)

    def mid_copy(d):
        t = peer(d)
        return remote(pack.at[t + 1], mid.at[i], mid_send.at[d], mid_recv.at[i], t, j)

    def edge_north():
        return remote(pack.at[n + 1], edge.at[i], edge_send.at[0], edge_recv.at[i], 0, after)

    def edge_south():
        return remote(pack.at[0], edge.at[i], edge_send.at[1], edge_recv.at[i], n - 1, before)

    order = list(range(n - 1, 0, -1))
    for d in order[:2]:
        main_copy(d).start()
    for load in loads:
        load.wait()
    sub = lax.broadcasted_iota(jnp.int32, (8, cells.shape[2]), 0)
    for u in range(n + 2):
        under, over = min(max(u - 2, 0), n - 1), min(u, n - 1)
        low = [pltpu.roll(tails[under, p].astype(jnp.float32), 2 + 2 * p, 0) for p in range(2)]
        high = [pltpu.roll(heads[over, p].astype(jnp.float32), 4 + p, 0) for p in range(2)]
        rows = jnp.where(sub < 2, low[0], jnp.where(sub < 4, low[1], jnp.where(sub == 4, high[0], high[1])))
        pack[u] = rows.astype(jnp.bfloat16)

    for d in order:
        mid_copy(d).start()

    @pl.when(j < m - 1)
    def _():
        edge_north().start()

    @pl.when(j > 0)
    def _():
        edge_south().start()

    for d in order[2:]:
        main_copy(d).start()
    own_mid = pltpu.make_async_copy(pack.at[i + 1], mid.at[i], own.at[1])
    own_mid.start()

    def edge_arrived(k):
        @pl.when(takes_south | takes_north)
        def _():
            remote(pack.at[0], edge.at[k], edge_send.at[0], edge_recv.at[k], i, after).wait_recv()

    first = arrival_stage(n, m, main, mid, edge, fields)
    own_main.wait()
    own_mid.wait()
    edge_arrived(i)
    first(i)
    for d in order:
        k = peer(d)
        remote(pack.at[0], mid.at[k], mid_send.at[d], mid_recv.at[k], k, j).wait_recv()
        edge_arrived(k)
        remote(rows_of(0), main.at[k], main_send.at[d], main_recv.at[k], k, j).wait_recv()
        first(k)

    for d in order:
        main_copy(d).wait_send()
        mid_copy(d).wait_send()

    @pl.when(j < m - 1)
    def _():
        edge_north().wait_send()

    @pl.when(j > 0)
    def _():
        edge_south().wait_send()


def parts(x0, y0, x1, y1):
    s0, s1 = x0 + y0, x1 + y1
    return x0 * y0 * s1 + x1 * y1 * s0, s0 * s1


def two_faces(one, two):
    scale = 2.0 / (one[1] * two[1])
    return one[0] * two[1] * scale, two[0] * one[1] * scale


def middle(one, two):
    x, y = one[0] * two[1], two[0] * one[1]
    total = 1.0 / (x + y)
    return x * total, y * total, 2.0 * (one[0] * two[0]) * total


def verticals(pairs):
    sums = [x + y for x, y in pairs]
    low, high = sums[0] * sums[1], sums[2] * sums[3]
    scale = 4.0 / (low * high)
    low, high = high * scale, low * scale
    shares = (sums[1] * low, sums[0] * low, sums[3] * high, sums[2] * high)
    return [x * y * share for (x, y), share in zip(pairs, shares)]


def arrival_stage(n, m, main, mid, edge, fields):
    band = main.shape[2]
    block = main.shape[3]
    half = band // 2
    rows = fields.shape[2]
    tiles = fields.shape[0] - 1
    per_block = block // (2 * LANES)
    i = lax.axis_index("gx")
    j = lax.axis_index("gy")
    last_rows = (i == n - 1) & (j == m - 1)

    taken = 2 * band + 16
    want = lax.broadcasted_iota(jnp.int32, (4 * rows, taken), 0)
    have = lax.broadcasted_iota(jnp.int32, (4 * rows, taken), 1)
    group = jnp.where(want >= 3 * rows, 3, jnp.where(want >= 2 * rows, 2, jnp.where(want >= rows, 1, 0)))
    place = want - group * rows
    plane = jnp.where(group >= 2, 1, 0)
    odd = group - 2 * plane
    inside = plane * band + 2 * jnp.where(place < half, place, 0) + odd
    above = jnp.where(odd == 0, 2 * band + jnp.where(i == n - 1, 8, 0) + 4 + plane, plane * band + 1)
    below = 2 * band + jnp.where(i == 0, 8, 0) + 2 * plane + odd
    source = jnp.where(place == half, above, jnp.where(place == rows - 1, below, inside))
    pick_rows = jnp.where(have == source, 1.0, 0.0).astype(jnp.bfloat16)
    fine = lax.broadcasted_iota(jnp.int32, (2 * LANES, 2 * LANES), 0)
    to = lax.broadcasted_iota(jnp.int32, (2 * LANES, 2 * LANES), 1)
    pick_cols = jnp.where(fine == jnp.where(to < LANES, 2 * to, 2 * (to - LANES) + 1), 1.0, 0.0).astype(jnp.bfloat16)

    top = (lax.broadcasted_iota(jnp.int32, (rows, LANES), 0) == half - 1) & last_rows

    def up(x):
        return pltpu.roll(x, rows - 1, 0)

    def tile_terms(k, part):
        t = k * per_block + part
        cols = pl.ds(pl.multiple_of(part * 2 * LANES, 2 * LANES), 2 * LANES)
        stored = jnp.concatenate(
            [
                main[k, 0, :, cols].astype(jnp.float32),
                main[k, 1, :, cols].astype(jnp.float32),
                mid[k, :, cols].astype(jnp.float32),
                edge[k, :, cols].astype(jnp.float32),
            ],
            axis=0,
        ).astype(jnp.bfloat16)
        picked = jnp.dot(pick_rows, stored, preferred_element_type=jnp.float32).astype(jnp.bfloat16)
        split = jnp.dot(picked, pick_cols, preferred_element_type=jnp.float32)
        a0, c0, a1, c1 = (split[g * rows : (g + 1) * rows, :LANES] for g in range(4))
        b0, d0, b1, d1 = (split[g * rows : (g + 1) * rows, LANES:] for g in range(4))
        def wall(x0, x1, inner):
            return jnp.where(top, 0.5 * (x0 + x1), inner[0]), jnp.where(top, 1.0, inner[1])

        s0, n0, t0 = middle(parts(a0, c0, a1, c1), wall(c0, c1, parts(c0, up(a0), c1, up(a1))))
        s1, n1, t1 = middle(parts(b0, d0, b1, d1), wall(d0, d1, parts(d0, up(b0), d1, up(b1))))
        h1, g1 = two_faces(parts(a0, b0, a1, b1), parts(c0, d0, c1, d1))
        pairs = ((a0, a1), (b0, b1), (c0, c1), (d0, d1))
        side_a, side_b, side_c, side_d = (
            (x + ((k0 + k1) + v)) - v for x, (k0, k1), v in zip((h1, h1, g1, g1), pairs, verticals(pairs))
        )
        for at, value in enumerate(
            (a0, a1, c0, c1, s0, n0, b0, b1, d0, d1, t0, s1, n1, t1, h1, g1, side_a, side_b, side_c, side_d)
        ):
            fields[t, at] = value

    def first(k):
        lax.fori_loop(0, per_block, lambda part, carry: (tile_terms(k, part), carry)[1], 0, unroll=UNROLL)

    ones = jnp.ones((rows, LANES), jnp.float32)
    for at in range(6):
        fields[tiles, at] = ones

    return first


def stencil_kernel(n, m, half, chunk, fields, out, held, sent):
    rows = fields.shape[2]
    tiles = fields.shape[0] - 1
    i = lax.axis_index("gx")
    j = lax.axis_index("gy")
    lane = lax.broadcasted_iota(jnp.int32, (rows, LANES), 1)
    sub = lax.broadcasted_iota(jnp.int32, (rows, LANES), 0)
    bottom = (sub == 0) & (i == 0) & (j == 0)
    top = (sub == half - 1) & (i == n - 1) & (j == m - 1)

    def up(x):
        return pltpu.roll(x, rows - 1, 0)

    def down(x):
        return pltpu.roll(x, 1, 0)

    def step(t, carry):
        last = (lane == LANES - 1) & (t == tiles - 1)
        first_lane = (lane == 0) & (t == 0)

        def ahead(at):
            return pltpu.roll(jnp.where(lane == 0, fields[t + 1, at], fields[t, at]), LANES - 1, 1)

        rolled = []

        def behind(x):
            turned = pltpu.roll(x, 1, 1)
            before = carry[len(rolled)]
            rolled.append(turned)
            return jnp.where(lane == 0, before, turned)

        a0, a1, c0, c1, s0, n0, b0, b1, d0, d1 = (fields[t, at] for at in range(10))
        t0, s1, n1, t1, h1, g1, side_a, side_b, side_c, side_d = (fields[t, at] for at in range(10, 20))
        wall_a, wall_b = a0 + a1, b0 + b1
        h2, g2 = two_faces(parts(b0, ahead(0), b1, ahead(1)), parts(d0, ahead(2), d1, ahead(3)))
        h2 = jnp.where(last, wall_b, h2)
        g2 = jnp.where(last, d0 + d1, g2)
        total = 1.0 / (h1 + h2)
        left, right = h1 * total, h2 * total
        left_up = up(left)
        right_up = up(right)
        s0_next = ahead(4)
        n0_next = ahead(5)
        side_a = side_a + jnp.where(first_lane, wall_a, behind(h2))
        side_c = side_c + jnp.where(first_lane, c0 + c1, behind(g2))
        side_b = side_b + h2
        side_d = side_d + g2

        nc = n0 * side_c
        sc = s0 * side_c
        nd = n1 * side_d
        sd = s1 * side_d
        even = side_a + t0 + s0 * sc + jnp.where(bottom, wall_a, down(t0 + n0 * nc))
        odd_ = side_b + t1 + s1 * sd + jnp.where(bottom, wall_b, down(t1 + n1 * nd))
        even_up = s0 * nc - t0
        odd_up = s1 * nd - t1
        sg = s0 * g1
        ng = n0 * g1
        sq = s0_next * g2
        nq = n0_next * g2
        p = h1 + s1 * sg + jnp.where(bottom, 0.0, down(n1 * ng))
        q = h2 + s1 * sq + jnp.where(bottom, 0.0, down(n1 * nq))
        p_up = n1 * sg
        p_down = s1 * ng
        q_up = s1 * nq
        q_down = n1 * sq

        mid = left * odd_ - p
        east = jnp.where(last, 0.0, right * mid - left * q)
        centre = even + left * (mid - p) + behind(right * (right * odd_ - 2.0 * q))
        lo = left * odd_up - p_up
        ro = right * odd_up - q_down
        north = even_up + left_up * lo - left * p_down + behind(right_up * ro - right * q_up)
        north = jnp.where(top, 0.0, north)
        north_east = jnp.where(last | top, 0.0, right_up * lo - left * q_up)
        north_west = jnp.where(last | top, 0.0, left_up * ro - right * p_down)
        west = behind(east)
        ne_back = behind(north_east)
        nw_back = behind(north_west)
        cols = pl.ds(pl.multiple_of(t * LANES, LANES), LANES)

        def below(x):
            return jnp.where(bottom, 0.0, down(x))

        for at, value in enumerate(
            (below(ne_back), below(north), below(north_west), west, centre, east, nw_back, north, north_east)
        ):
            held[at, :, cols] = value[:half]
        return tuple(rolled)

    def leave(c):
        cols = pl.ds(c * chunk * LANES, chunk * LANES)
        return pltpu.make_async_copy(held.at[:, :, cols], out.at[:, :, cols], sent.at[c])

    carry = (jnp.zeros((rows, LANES), jnp.float32),) * 7
    for c in range(tiles // chunk):
        carry = lax.fori_loop(c * chunk, (c + 1) * chunk, step, carry, unroll=STEPS)
        leave(c).start()
    for c in range(tiles // chunk):
        leave(c).wait()


def shards(n, m, conductivity):
    planes, local_rows, local_cols = conductivity.shape
    band = local_rows // n
    half = band // 2
    rows = -(-(half + 2) // 8) * 8
    tiles = n * local_cols // (2 * LANES)
    vmem = pl.BlockSpec(memory_space=pltpu.VMEM)
    anywhere = pl.BlockSpec(memory_space=pl.ANY)
    dma = pltpu.SemaphoreType.DMA
    shape = (tiles + 1, 20, rows, LANES)
    fields = pl.pallas_call(
        functools.partial(coarse_kernel, n, m),
        out_shape=jax.ShapeDtypeStruct(shape, jnp.float32),
        in_specs=[anywhere],
        out_specs=vmem,
        scratch_shapes=[
            pltpu.VMEM((n, planes, band, local_cols), jnp.bfloat16),
            pltpu.VMEM((n, 8, local_cols), jnp.bfloat16),
            pltpu.VMEM((n, 8, local_cols), jnp.bfloat16),
            pltpu.VMEM((n, planes, 8, local_cols), jnp.bfloat16),
            pltpu.VMEM((n, planes, 8, local_cols), jnp.bfloat16),
            pltpu.VMEM((n + 2, 8, local_cols), jnp.bfloat16),
            dma((n,)),
            dma((n,)),
            dma((n,)),
            dma((n,)),
            dma((2,)),
            dma((n,)),
            dma((2 * n + 1,)),
        ],
        compiler_params=pltpu.CompilerParams(
            collective_id=0, has_side_effects=True, vmem_limit_bytes=VMEM_LIMIT
        ),
        name="coarse",
    )(pltpu.with_memory_space_constraint(conductivity, pltpu.HBM))
    chunk = tiles // 4
    stencil = pl.pallas_call(
        functools.partial(stencil_kernel, n, m, half, chunk),
        out_shape=jax.ShapeDtypeStruct((9, half, tiles * LANES), jnp.float32),
        in_specs=[vmem],
        out_specs=anywhere,
        scratch_shapes=[pltpu.VMEM((9, half, tiles * LANES), jnp.float32), dma((4,))],
        compiler_params=pltpu.CompilerParams(vmem_limit_bytes=VMEM_LIMIT),
        name="stencil",
    )(fields)
    return stencil[:, None]


def solution(mesh):
    n, m = mesh.shape["gx"], mesh.shape["gy"]
    return jax.shard_map(
        functools.partial(shards, n, m),
        mesh=mesh,
        in_specs=(P(None, "gy", "gx"),),
        out_specs=P(None, "gy", "gx", None),
        check_vma=False,
    )
```

```python
import functools

import jax
import jax.numpy as jnp
from jax import lax
from jax.experimental import pallas as pl
from jax.experimental.pallas import tpu as pltpu
from jax.sharding import PartitionSpec as P

MESH = pl.DeviceIdType.MESH
LANES = 128
UNROLL = 4
STEPS = 4
VMEM_LIMIT = 16 * 1024 * 1024


def coarse_kernel(
    n, m, cells, fields, main, mid, edge, tails, heads, pack,
    main_send, main_recv, mid_send, mid_recv, edge_send, edge_recv, own,
):
    i = lax.axis_index("gx")
    j = lax.axis_index("gy")
    band = main.shape[2]
    takes_south = (i == 0) & (j > 0)
    takes_north = (i == n - 1) & (j < m - 1)
    before = jnp.maximum(j - 1, 0)
    after = jnp.minimum(j + 1, m - 1)

    barrier = pltpu.get_barrier_semaphore()

    def greet(x, y):
        pl.semaphore_signal(barrier, inc=1, device_id=(x, y), device_id_type=MESH)

    for d in range(1, n):
        greet(lax.rem(i + d, n), j)

    @pl.when(takes_south)
    def _():
        for k in range(n):
            greet(k, before)

    @pl.when(takes_north)
    def _():
        for k in range(n):
            greet(k, after)

    def rows_of(t):
        return cells.at[:, pl.ds(pl.multiple_of(t * band, band), band), :]

    own_main = pltpu.make_async_copy(rows_of(i), main.at[i], own.at[2 * n])
    own_main.start()

    loads = []
    for t in range(n):
        loads.append(pltpu.make_async_copy(cells.at[:, pl.ds(t * band + band - 8, 8), :], tails.at[t], own.at[2 * t]))
        loads.append(pltpu.make_async_copy(cells.at[:, pl.ds(t * band, 8), :], heads.at[t], own.at[2 * t + 1]))
    for load in loads:
        load.start()
    @pl.when(jnp.logical_not(takes_south | takes_north))
    def _():
        edge[...] = jnp.ones(edge.shape, edge.dtype)

    north, south = jnp.where(j < m - 1, 1, 0), jnp.where(j > 0, 1, 0)
    pl.semaphore_wait(barrier, n - 1 + north + south)

    def remote(src, dst, send, recv, x, y):
        return pltpu.make_async_remote_copy(
            src_ref=src, dst_ref=dst, send_sem=send, recv_sem=recv, device_id=(x, y), device_id_type=MESH
        )

    near = jnp.where(i < n // 2, i, n - 1 - i)

    def peer(d):
        t = jnp.where(d > near, d, d - 1)
        return jnp.where(i < n // 2, t, n - 1 - t)

    def main_copy(d):
        t = peer(d)
        return remote(rows_of(t), main.at[i], main_send.at[d], main_recv.at[i], t, j)

    def mid_copy(d):
        t = peer(d)
        return remote(pack.at[t + 1], mid.at[i], mid_send.at[d], mid_recv.at[i], t, j)

    def edge_north():
        return remote(pack.at[n + 1], edge.at[i], edge_send.at[0], edge_recv.at[i], 0, after)

    def edge_south():
        return remote(pack.at[0], edge.at[i], edge_send.at[1], edge_recv.at[i], n - 1, before)

    order = list(range(n - 1, 0, -1))
    for d in order[:2]:
        main_copy(d).start()
    for load in loads:
        load.wait()
    sub = lax.broadcasted_iota(jnp.int32, (8, cells.shape[2]), 0)
    for u in range(n + 2):
        under, over = min(max(u - 2, 0), n - 1), min(u, n - 1)
        low = [pltpu.roll(tails[under, p].astype(jnp.float32), 2 + 2 * p, 0) for p in range(2)]
        high = [pltpu.roll(heads[over, p].astype(jnp.float32), 4 + p, 0) for p in range(2)]
        rows = jnp.where(sub < 2, low[0], jnp.where(sub < 4, low[1], jnp.where(sub == 4, high[0], high[1])))
        pack[u] = rows.astype(jnp.bfloat16)

    for d in order:
        mid_copy(d).start()

    @pl.when(j < m - 1)
    def _():
        edge_north().start()

    @pl.when(j > 0)
    def _():
        edge_south().start()

    for d in order[2:]:
        main_copy(d).start()
    own_mid = pltpu.make_async_copy(pack.at[i + 1], mid.at[i], own.at[1])
    own_mid.start()

    def edge_arrived(k):
        @pl.when(takes_south | takes_north)
        def _():
            remote(pack.at[0], edge.at[k], edge_send.at[0], edge_recv.at[k], i, after).wait_recv()

    first = arrival_stage(n, m, main, mid, edge, fields)
    own_main.wait()
    own_mid.wait()
    edge_arrived(i)
    first(i)
    for d in order:
        k = peer(d)
        remote(pack.at[0], mid.at[k], mid_send.at[d], mid_recv.at[k], k, j).wait_recv()
        edge_arrived(k)
        remote(rows_of(0), main.at[k], main_send.at[d], main_recv.at[k], k, j).wait_recv()
        first(k)

    for d in order:
        main_copy(d).wait_send()
        mid_copy(d).wait_send()

    @pl.when(j < m - 1)
    def _():
        edge_north().wait_send()

    @pl.when(j > 0)
    def _():
        edge_south().wait_send()


def parts(x0, y0, x1, y1):
    s0, s1 = x0 + y0, x1 + y1
    return x0 * y0 * s1 + x1 * y1 * s0, s0 * s1


def two_faces(one, two):
    scale = 2.0 / (one[1] * two[1])
    return one[0] * two[1] * scale, two[0] * one[1] * scale


def middle(one, two):
    x, y = one[0] * two[1], two[0] * one[1]
    total = 1.0 / (x + y)
    return x * total, y * total, 2.0 * (one[0] * two[0]) * total


def verticals(pairs):
    sums = [x + y for x, y in pairs]
    low, high = sums[0] * sums[1], sums[2] * sums[3]
    scale = 4.0 / (low * high)
    low, high = high * scale, low * scale
    shares = (sums[1] * low, sums[0] * low, sums[3] * high, sums[2] * high)
    return [x * y * share for (x, y), share in zip(pairs, shares)]


def arrival_stage(n, m, main, mid, edge, fields):
    band = main.shape[2]
    block = main.shape[3]
    half = band // 2
    rows = fields.shape[2]
    tiles = fields.shape[0] - 1
    per_block = block // (2 * LANES)
    i = lax.axis_index("gx")
    j = lax.axis_index("gy")
    last_rows = (i == n - 1) & (j == m - 1)

    taken = 2 * band + 16
    want = lax.broadcasted_iota(jnp.int32, (4 * rows, taken), 0)
    have = lax.broadcasted_iota(jnp.int32, (4 * rows, taken), 1)
    group = jnp.where(want >= 3 * rows, 3, jnp.where(want >= 2 * rows, 2, jnp.where(want >= rows, 1, 0)))
    place = want - group * rows
    plane = jnp.where(group >= 2, 1, 0)
    odd = group - 2 * plane
    inside = plane * band + 2 * jnp.where(place < half, place, 0) + odd
    above = jnp.where(odd == 0, 2 * band + jnp.where(i == n - 1, 8, 0) + 4 + plane, plane * band + 1)
    below = 2 * band + jnp.where(i == 0, 8, 0) + 2 * plane + odd
    source = jnp.where(place == half, above, jnp.where(place == rows - 1, below, inside))
    pick_rows = jnp.where(have == source, 1.0, 0.0).astype(jnp.bfloat16)
    fine = lax.broadcasted_iota(jnp.int32, (2 * LANES, 2 * LANES), 0)
    to = lax.broadcasted_iota(jnp.int32, (2 * LANES, 2 * LANES), 1)
    pick_cols = jnp.where(fine == jnp.where(to < LANES, 2 * to, 2 * (to - LANES) + 1), 1.0, 0.0).astype(jnp.bfloat16)

    top = (lax.broadcasted_iota(jnp.int32, (rows, LANES), 0) == half - 1) & last_rows

    def up(x):
        return pltpu.roll(x, rows - 1, 0)

    def tile_terms(k, part):
        t = k * per_block + part
        cols = pl.ds(pl.multiple_of(part * 2 * LANES, 2 * LANES), 2 * LANES)
        stored = jnp.concatenate(
            [
                main[k, 0, :, cols].astype(jnp.float32),
                main[k, 1, :, cols].astype(jnp.float32),
                mid[k, :, cols].astype(jnp.float32),
                edge[k, :, cols].astype(jnp.float32),
            ],
            axis=0,
        ).astype(jnp.bfloat16)
        picked = jnp.dot(pick_rows, stored, preferred_element_type=jnp.float32).astype(jnp.bfloat16)
        split = jnp.dot(picked, pick_cols, preferred_element_type=jnp.float32)
        a0, c0, a1, c1 = (split[g * rows : (g + 1) * rows, :LANES] for g in range(4))
        b0, d0, b1, d1 = (split[g * rows : (g + 1) * rows, LANES:] for g in range(4))
        def wall(x0, x1, inner):
            return jnp.where(top, 0.5 * (x0 + x1), inner[0]), jnp.where(top, 1.0, inner[1])

        s0, n0, t0 = middle(parts(a0, c0, a1, c1), wall(c0, c1, parts(c0, up(a0), c1, up(a1))))
        s1, n1, t1 = middle(parts(b0, d0, b1, d1), wall(d0, d1, parts(d0, up(b0), d1, up(b1))))
        h1, g1 = two_faces(parts(a0, b0, a1, b1), parts(c0, d0, c1, d1))
        pairs = ((a0, a1), (b0, b1), (c0, c1), (d0, d1))
        side_a, side_b, side_c, side_d = (
            (x + ((k0 + k1) + v)) - v for x, (k0, k1), v in zip((h1, h1, g1, g1), pairs, verticals(pairs))
        )
        for at, value in enumerate(
            (a0, a1, c0, c1, s0, n0, b0, b1, d0, d1, t0, s1, n1, t1, h1, g1, side_a, side_b, side_c, side_d)
        ):
            fields[t, at] = value

    def first(k):
        lax.fori_loop(0, per_block, lambda part, carry: (tile_terms(k, part), carry)[1], 0, unroll=UNROLL)

    ones = jnp.ones((rows, LANES), jnp.float32)
    for at in range(6):
        fields[tiles, at] = ones

    return first


def stencil_kernel(n, m, half, chunk, fields, out, held, sent):
    rows = fields.shape[2]
    tiles = fields.shape[0] - 1
    i = lax.axis_index("gx")
    j = lax.axis_index("gy")
    lane = lax.broadcasted_iota(jnp.int32, (rows, LANES), 1)
    sub = lax.broadcasted_iota(jnp.int32, (rows, LANES), 0)
    bottom = (sub == 0) & (i == 0) & (j == 0)
    top = (sub == half - 1) & (i == n - 1) & (j == m - 1)

    def up(x):
        return pltpu.roll(x, rows - 1, 0)

    def down(x):
        return pltpu.roll(x, 1, 0)

    def step(t, carry):
        last = (lane == LANES - 1) & (t == tiles - 1)
        first_lane = (lane == 0) & (t == 0)

        def ahead(at):
            return pltpu.roll(jnp.where(lane == 0, fields[t + 1, at], fields[t, at]), LANES - 1, 1)

        rolled = []

        def behind(x):
            turned = pltpu.roll(x, 1, 1)
            before = carry[len(rolled)]
            rolled.append(turned)
            return jnp.where(lane == 0, before, turned)

        a0, a1, c0, c1, s0, n0, b0, b1, d0, d1 = (fields[t, at] for at in range(10))
        t0, s1, n1, t1, h1, g1, side_a, side_b, side_c, side_d = (fields[t, at] for at in range(10, 20))
        wall_a, wall_b = a0 + a1, b0 + b1
        h2, g2 = two_faces(parts(b0, ahead(0), b1, ahead(1)), parts(d0, ahead(2), d1, ahead(3)))
        h2 = jnp.where(last, wall_b, h2)
        g2 = jnp.where(last, d0 + d1, g2)
        total = 1.0 / (h1 + h2)
        left, right = h1 * total, h2 * total
        left_up = up(left)
        right_up = up(right)
        s0_next = ahead(4)
        n0_next = ahead(5)
        side_a = side_a + jnp.where(first_lane, wall_a, behind(h2))
        side_c = side_c + jnp.where(first_lane, c0 + c1, behind(g2))
        side_b = side_b + h2
        side_d = side_d + g2

        nc = n0 * side_c
        sc = s0 * side_c
        nd = n1 * side_d
        sd = s1 * side_d
        even = side_a + t0 + s0 * sc + jnp.where(bottom, wall_a, down(t0 + n0 * nc))
        odd_ = side_b + t1 + s1 * sd + jnp.where(bottom, wall_b, down(t1 + n1 * nd))
        even_up = s0 * nc - t0
        odd_up = s1 * nd - t1
        sg = s0 * g1
        ng = n0 * g1
        sq = s0_next * g2
        nq = n0_next * g2
        p = h1 + s1 * sg + jnp.where(bottom, 0.0, down(n1 * ng))
        q = h2 + s1 * sq + jnp.where(bottom, 0.0, down(n1 * nq))
        p_up = n1 * sg
        p_down = s1 * ng
        q_up = s1 * nq
        q_down = n1 * sq

        mid = left * odd_ - p
        east = jnp.where(last, 0.0, right * mid - left * q)
        centre = even + left * (mid - p) + behind(right * (right * odd_ - 2.0 * q))
        lo = left * odd_up - p_up
        ro = right * odd_up - q_down
        north = even_up + left_up * lo - left * p_down + behind(right_up * ro - right * q_up)
        north = jnp.where(top, 0.0, north)
        north_east = jnp.where(last | top, 0.0, right_up * lo - left * q_up)
        north_west = jnp.where(last | top, 0.0, left_up * ro - right * p_down)
        west = behind(east)
        ne_back = behind(north_east)
        nw_back = behind(north_west)
        cols = pl.ds(pl.multiple_of(t * LANES, LANES), LANES)

        def below(x):
            return jnp.where(bottom, 0.0, down(x))

        for at, value in enumerate(
            (below(ne_back), below(north), below(north_west), west, centre, east, nw_back, north, north_east)
        ):
            held[at, :, cols] = value[:half]
        return tuple(rolled)

    def leave(c):
        cols = pl.ds(c * chunk * LANES, chunk * LANES)
        return pltpu.make_async_copy(held.at[:, :, cols], out.at[:, :, cols], sent.at[c])

    carry = (jnp.zeros((rows, LANES), jnp.float32),) * 7
    for c in range(tiles // chunk):
        carry = lax.fori_loop(c * chunk, (c + 1) * chunk, step, carry, unroll=STEPS)
        leave(c).start()
    for c in range(tiles // chunk):
        leave(c).wait()


def shards(n, m, conductivity):
    planes, local_rows, local_cols = conductivity.shape
    band = local_rows // n
    half = band // 2
    rows = -(-(half + 2) // 8) * 8
    tiles = n * local_cols // (2 * LANES)
    vmem = pl.BlockSpec(memory_space=pltpu.VMEM)
    anywhere = pl.BlockSpec(memory_space=pl.ANY)
    dma = pltpu.SemaphoreType.DMA
    shape = (tiles + 1, 20, rows, LANES)
    fields = pl.pallas_call(
        functools.partial(coarse_kernel, n, m),
        out_shape=jax.ShapeDtypeStruct(shape, jnp.float32),
        in_specs=[anywhere],
        out_specs=vmem,
        scratch_shapes=[
            pltpu.VMEM((n, planes, band, local_cols), jnp.bfloat16),
            pltpu.VMEM((n, 8, local_cols), jnp.bfloat16),
            pltpu.VMEM((n, 8, local_cols), jnp.bfloat16),
            pltpu.VMEM((n, planes, 8, local_cols), jnp.bfloat16),
            pltpu.VMEM((n, planes, 8, local_cols), jnp.bfloat16),
            pltpu.VMEM((n + 2, 8, local_cols), jnp.bfloat16),
            dma((n,)),
            dma((n,)),
            dma((n,)),
            dma((n,)),
            dma((2,)),
            dma((n,)),
            dma((2 * n + 1,)),
        ],
        compiler_params=pltpu.CompilerParams(
            collective_id=0, has_side_effects=True, vmem_limit_bytes=VMEM_LIMIT
        ),
        name="coarse",
    )(pltpu.with_memory_space_constraint(conductivity, pltpu.HBM))
    chunk = tiles // 4
    stencil = pl.pallas_call(
        functools.partial(stencil_kernel, n, m, half, chunk),
        out_shape=jax.ShapeDtypeStruct((9, half, tiles * LANES), jnp.float32),
        in_specs=[vmem],
        out_specs=anywhere,
        scratch_shapes=[pltpu.VMEM((9, half, tiles * LANES), jnp.float32), dma((4,))],
        compiler_params=pltpu.CompilerParams(vmem_limit_bytes=VMEM_LIMIT),
        name="stencil",
    )(fields)
    return stencil[:, None]


def solution(mesh):
    n, m = mesh.shape["gx"], mesh.shape["gy"]
    return jax.shard_map(
        functools.partial(shards, n, m),
        mesh=mesh,
        in_specs=(P(None, "gy", "gx"),),
        out_specs=P(None, "gy", "gx", None),
        check_vma=False,
    )
```
